32 devices in a mesh: parts: 2 (over x), context: 8 (over z, core), tensor: 2 (over y).
Axes of the slice: x: 2, y: 2, z: 4, core: 2. Of those that a mesh axis runs over, the one named last changes fastest.
Arguments:
- queries: bfloat16 [4096, 8192], P(('parts', 'context'), 'tensor'), parts along dimension 0, may hold values from -13 to 13
- keys: bfloat16 [4096, 1024], P(('parts', 'context'), 'tensor'), parts along dimension 0, may hold values from -5.2 to 5.2
- values: bfloat16 [4096, 1024], P(('parts', 'context'), 'tensor'), parts along dimension 0, may hold values from -6 to 6
- out_weight: bfloat16 [8192, 4096], P('tensor'), may hold values from -0.1875 to 0.1875
Outputs:
- mixed: bfloat16 [4096, 4096], P(('parts', 'context'), 'tensor'), parts along dimension 0
The draws below stay inside these ranges and needn't reach their ends.
There are 2 independent parts, one for each index of `parts`. The reference program is written for one: setup_inputs(seed, part) draws one part's arguments, and reference() takes and returns one part's arrays. A program takes and returns all parts, laid end to end along the dimension named above; an argument that names none is the same for every part. Nothing has to cross between parts.
All inputs are finite; a program needn't handle non-finite values.
Results may differ from the reference program's by a relative error of at most 0.015.
Values may be sent and summed in bfloat16 or wider, within the bound.
A program may use at most 128 MiB of HBM per device.

```python
import jax
import jax.numpy as jnp
from jax import lax

D = 4096
HD = 128
HQ = 64
KVH = 8
TOKENS = 2048
N_TENSOR = 2


def draw_common(key):
    key_base = jnp.clip(jax.random.normal(jax.random.fold_in(key, 21), (TOKENS, KVH * HD), jnp.float32), -4.0, 4.0)
    query_base = jnp.clip(2.5 * jax.random.normal(jax.random.fold_in(key, 22), (TOKENS, HQ * HD), jnp.float32), -10.0, 10.0)
    return (query_base, key_base)


def draw_queries(key, part):
    query_base, key_base = draw_common(key)
    return query_base.astype(jnp.bfloat16)


def draw_keys(key, part):
    query_base, key_base = draw_common(key)
    return key_base.astype(jnp.bfloat16)


def levels(own_key, shape, shards, low, top_value):
    loudness, own = 1.0, jax.random.fold_in(own_key, 6)
    for position, shards_of in shards:
        steps = jnp.exp(jax.random.uniform(jax.random.fold_in(own, position), (shards_of,), jnp.float32, low / len(shards), top_value / len(shards)))
        loudness = loudness * jnp.repeat(steps, shape[position] // shards_of).reshape([-1 if axis == position else 1 for axis in range(len(shape))])
    return loudness


def gaussian(own_key, dims, scale, bound, split=(), kind=jnp.bfloat16):
    array = jax.random.normal(own_key, dims, jnp.float32) * scale
    if len(split) > 0:
        array = levels(own_key, dims, split, -0.22, 0.18) * array
    return jnp.clip(array, min=-bound, max=bound).astype(kind)


def setup_inputs(seed: int = 0, part: int = 0) -> dict:
    streams_of = jax.random.split(jax.random.key(seed), 5)
    part_splits = jax.random.split(jax.random.fold_in(streams_of[4], part), 5)
    return {
        "queries": draw_queries(jax.random.fold_in(jax.random.fold_in(streams_of[4], part), 71), part),
        "keys": draw_keys(jax.random.fold_in(jax.random.fold_in(streams_of[4], part), 71), part),
        "values": gaussian(part_splits[2], (TOKENS, KVH * HD), 1.0, 6.0, ((0, 8), (1, 2))),
        "out_weight": gaussian(streams_of[3], (HQ * HD, D), (HQ * HD // 8) ** -0.5, 0.1875, ((0, 2),)),
    }


def reference(queries, keys, values, out_weight):
    tok_count = queries.shape[0]
    group_size = HQ // KVH
    query_heads = queries.reshape(tok_count, HQ, HD).transpose(1, 0, 2)
    key_heads = keys.reshape(tok_count, KVH, HD).transpose(1, 0, 2)
    value_heads = values.reshape(tok_count, KVH, HD).transpose(1, 0, 2)
    positions = jnp.arange(tok_count, dtype=jnp.int32)
    visible = positions[None, :] <= positions[:, None]

    def one_head(head_idx):
        kv_idx = head_idx // group_size
        query_mat = query_heads[head_idx]
        key_mat = key_heads[kv_idx]
        value_mat = value_heads[kv_idx]
        scores = jnp.dot(query_mat, key_mat.T, preferred_element_type=jnp.float32) * (HD ** -0.5)
        scores = jnp.where(visible, scores, -jnp.inf)
        top_val = jnp.max(scores, axis=1, keepdims=True)
        expo = jnp.exp(scores - top_val)
        totals = jnp.sum(expo, axis=1, keepdims=True)
        mixed_head = jnp.dot(expo.astype(jnp.bfloat16), value_mat, preferred_element_type=jnp.float32) / totals
        return mixed_head.astype(jnp.bfloat16)

    head_outs = lax.map(one_head, jnp.arange(HQ, dtype=jnp.int32))
    attended = head_outs.transpose(1, 0, 2).reshape(tok_count, HQ * HD)
    width_share = HQ * HD // N_TENSOR
    summed = jnp.zeros((tok_count, D), jnp.float32)
    for group_idx in range(N_TENSOR):
        cols = attended[:, group_idx * width_share:(group_idx + 1) * width_share]
        rows_part = out_weight[group_idx * width_share:(group_idx + 1) * width_share]
        partial_value = jnp.dot(cols, rows_part, preferred_element_type=jnp.float32)
        rounded = lax.optimization_barrier(partial_value.astype(jnp.bfloat16))
        summed = summed + rounded.astype(jnp.float32)
    return summed.astype(jnp.bfloat16)
```

```python
import functools

import jax
import jax.numpy as jnp
import numpy as np
from jax import lax
from jax.experimental import pallas as pl
from jax.experimental.pallas import tpu as pltpu
from jax.sharding import PartitionSpec as P

HD = 128
F32 = jnp.float32
BF16 = jnp.bfloat16


def kernel(dims, q_hbm, k_hbm, v_hbm, w_hbm, out_ref,
           qs, kvg, wv, acc, top, att, sendbuf, recvbuf,
           q_sem, kv_sem, w_sem, zs_sem, ss_sem, zr_sem, sr_sem, ys_sem, yr_sem):
    C, N, tok, n_kv, group, n_out, width, n_chunk, rows = dims
    c = lax.axis_index("context")
    t = lax.axis_index("tensor")
    z = c // 2
    odd = c % 2
    sibling = c + 1 - 2 * odd
    has_up = c + 2 < C
    has_down = c >= 2
    factor = float(HD ** -0.5 * np.log2(np.e))
    tiles = group * tok // rows

    def block(kv, b):
        return kvg.at[kv, pl.ds(pl.multiple_of(b * tok, tok), tok), :]

    own = [pltpu.make_async_copy(k_hbm, block(0, c), kv_sem.at[0]),
           pltpu.make_async_copy(v_hbm, block(1, c), kv_sem.at[1])]
    for copy in own:
        copy.start()

    def q_copy(h):
        return pltpu.make_async_copy(
            q_hbm.at[:, pl.ds(pl.multiple_of(h * HD, HD), HD)],
            qs.at[h // group, pl.ds(pl.multiple_of((h % group) * tok, tok), tok), :],
            q_sem.at[h])

    @pl.loop(0, n_kv * group)
    def _(h):
        q_copy(h).start()

    barrier = pltpu.get_barrier_semaphore()
    pl.semaphore_signal(barrier, inc=1, device_id={"context": sibling})

    @pl.when(has_up)
    def _():
        pl.semaphore_signal(barrier, inc=1, device_id={"context": c + 2})

    @pl.when(has_down)
    def _():
        pl.semaphore_signal(barrier, inc=1, device_id={"context": c - 2})

    for d in range(1, N):
        pl.semaphore_signal(barrier, inc=1, device_id={"tensor": lax.rem(t + d, N)})
    pl.semaphore_wait(barrier, N + has_up.astype(jnp.int32) + has_down.astype(jnp.int32))

    def up_copy(kv, b):
        return pltpu.make_async_remote_copy(
            src_ref=block(kv, b), dst_ref=block(kv, b),
            send_sem=zs_sem.at[kv, b], recv_sem=zr_sem.at[kv, b],
            device_id={"context": c + 2})

    def side_copy(kv, b):
        return pltpu.make_async_remote_copy(
            src_ref=block(kv, b), dst_ref=block(kv, b),
            send_sem=ss_sem.at[kv, b], recv_sem=sr_sem.at[kv, b],
            device_id={"context": sibling})

    for kv in range(2):
        own[kv].wait()

        @pl.when(has_up)
        def _():
            up_copy(kv, c).start()

        @pl.when(odd == 0)
        def _():
            side_copy(kv, c).start()

    def w_copy(i):
        cols = pl.ds(pl.multiple_of(i * width, width), width)
        return pltpu.make_async_copy(w_hbm.at[:, cols], wv.at[:, cols], w_sem.at[i])

    @pl.loop(0, N * n_chunk)
    def _(i):
        w_copy(i).start()

    @pl.loop(0, n_kv * group)
    def _(h):
        q_copy(h).wait()

    def attend(row0, n_keys, first):
        row0 = pl.multiple_of(row0, tok)

        @pl.loop(0, n_kv * tiles)
        def _(i):
            head = i // tiles
            here = pl.ds(pl.multiple_of((i % tiles) * rows, rows), rows)
            lanes = pl.ds(pl.multiple_of(head * HD, HD), HD)
            key = kvg[0, pl.ds(row0, n_keys), lanes]
            val = kvg[1, pl.ds(row0, n_keys), lanes]
            s = lax.dot_general(qs[head, here, :], key, (((1,), (1,)), ((), ())),
                                preferred_element_type=F32)
            if first:
                r = lax.broadcasted_iota(jnp.int32, s.shape, 0) % tok
                k = lax.broadcasted_iota(jnp.int32, s.shape, 1)
                s = jnp.where(k <= r, s, -1e30)
            parts = [s[:, j * HD:(j + 1) * HD] for j in range(n_keys // HD)]
            m = functools.reduce(jnp.maximum, parts)
            m = jnp.broadcast_to(jnp.max(m, axis=1, keepdims=True), m.shape)
            if not first:
                before = top[head, here, :]
                m = jnp.maximum(before, m)
                shrink = jnp.exp2((before - m) * factor)
            top[head, here, :] = m
            mf = m * factor
            p = jnp.concatenate([jnp.exp2(x * factor - mf).astype(BF16) for x in parts], axis=1)
            both = jnp.concatenate([val, jnp.ones_like(val)], axis=1)
            pv = jnp.dot(p, both, preferred_element_type=F32)
            if not first:
                pv = acc[head, here, :] * jnp.concatenate([shrink, shrink], axis=1) + pv
            acc[head, here, :] = pv

    attend(c * tok, tok, True)

    @pl.when(odd == 1)
    def _():
        for kv in range(2):
            side_copy(kv, sibling).wait_recv()
        attend(sibling * tok, tok, False)

    @pl.loop(1, z + 1)
    def _(i):
        b = c - 2 * i
        for kv in range(2):
            up_copy(kv, b).wait_recv()

            @pl.when(has_up)
            def _():
                up_copy(kv, b).start()

            side_copy(kv, b).start()
        for kv in range(2):
            side_copy(kv, sibling - 2 * i).wait_recv()
        attend((z - i) * 2 * tok, 2 * tok, False)

    @pl.loop(0, n_kv * group)
    def _(h):
        here = pl.ds(pl.multiple_of((h % group) * tok, tok), tok)
        a = acc[h // group, here, :]
        att[:, pl.ds(pl.multiple_of(h * HD, HD), HD)] = (a[:, :HD] / a[:, HD:]).astype(BF16)

    def y_copy(i):
        d = i // n_chunk + 1
        return pltpu.make_async_remote_copy(
            src_ref=sendbuf.at[i], dst_ref=recvbuf.at[i],
            send_sem=ys_sem.at[i], recv_sem=yr_sem.at[i],
            device_id={"tensor": lax.rem(t + d, N)})

    def project(chunk):
        w_copy(chunk).wait()
        cols = pl.ds(pl.multiple_of(chunk * width, width), width)
        return jnp.dot(att[...], wv[:, cols], preferred_element_type=F32).astype(BF16)

    @pl.loop(0, (N - 1) * n_chunk)
    def _(i):
        peer = lax.rem(t + i // n_chunk + 1, N)
        sendbuf[i] = project(peer * n_chunk + i % n_chunk)
        y_copy(i).start()

    @pl.loop(0, n_chunk)
    def _(j):
        total = project(t * n_chunk + j).astype(F32)
        for d in range(N - 1):
            y_copy(d * n_chunk + j).wait_recv()
            total = total + recvbuf[d * n_chunk + j].astype(F32)
        out_ref[:, pl.ds(pl.multiple_of(j * width, width), width)] = total.astype(BF16)

    @pl.loop(0, (N - 1) * n_chunk)
    def _(i):
        y_copy(i).wait_send()

    @pl.when(has_up)
    def _():
        @pl.loop(0, z + 1)
        def _(i):
            for kv in range(2):
                up_copy(kv, c - 2 * i).wait_send()

    @pl.loop(1 - (odd == 0).astype(jnp.int32), z + 1)
    def _(i):
        for kv in range(2):
            side_copy(kv, c - 2 * i).wait_send()


def body(C, N, queries, keys, values, out_weight):
    tok, q_width = queries.shape
    kv_width = keys.shape[1]
    n_kv = kv_width // HD
    group = q_width // kv_width
    n_feat, n_out = out_weight.shape
    own_width = n_out // N
    width = min(512, own_width)
    n_chunk = own_width // width
    rows = 2 * tok
    dims = (C, N, tok, n_kv, group, n_out, width, n_chunk, rows)
    n_send = (N - 1) * n_chunk
    dma = pltpu.SemaphoreType.DMA
    return pl.pallas_call(
        functools.partial(kernel, dims),
        out_shape=jax.ShapeDtypeStruct((tok, own_width), BF16),
        in_specs=[pl.BlockSpec(memory_space=pl.ANY)] * 4,
        out_specs=pl.BlockSpec(memory_space=pltpu.VMEM),
        scratch_shapes=[
            pltpu.VMEM((n_kv, group * tok, HD), BF16),
            pltpu.VMEM((2, C * tok, kv_width), BF16),
            pltpu.VMEM((n_feat, n_out), BF16),
            pltpu.VMEM((n_kv, group * tok, 2 * HD), F32),
            pltpu.VMEM((n_kv, group * tok, HD), F32),
            pltpu.VMEM((tok, q_width), BF16),
            pltpu.VMEM((n_send, tok, width), BF16),
            pltpu.VMEM((n_send, tok, width), BF16),
            dma((n_kv * group,)),
            dma((2,)),
            dma((N * n_chunk,)),
            dma((2, C)),
            dma((2, C)),
            dma((2, C)),
            dma((2, C)),
            dma((n_send,)),
            dma((n_send,)),
        ],
        compiler_params=pltpu.CompilerParams(
            collective_id=0, has_side_effects=True, vmem_limit_bytes=67043328
        ),
    )(queries, keys, values, out_weight)


def solution(mesh):
    C, N = mesh.shape["context"], mesh.shape["tensor"]
    return jax.shard_map(
        functools.partial(body, C, N),
        mesh=mesh,
        in_specs=(
            P(("parts", "context"), "tensor"),
            P(("parts", "context"), "tensor"),
            P(("parts", "context"), "tensor"),
            P("tensor", None),
        ),
        out_specs=P(("parts", "context"), "tensor"),
        check_vma=False,
    )
```

```python
import functools

import jax
import jax.numpy as jnp
import numpy as np
from jax import lax
from jax.experimental import pallas as pl
from jax.experimental.pallas import tpu as pltpu
from jax.sharding import PartitionSpec as P

HD = 128
F32 = jnp.float32
BF16 = jnp.bfloat16


def kernel(dims, q_hbm, k_hbm, v_hbm, w_hbm, out_ref,
           qs, kvg, wv, acc, top, att, sendbuf, recvbuf,
           q_sem, kv_sem, w_sem, zs_sem, ss_sem, zr_sem, sr_sem, ys_sem, yr_sem):
    C, N, tok, n_kv, group, n_out, width, n_chunk = dims
    c = lax.axis_index("context")
    t = lax.axis_index("tensor")
    z = c // 2
    odd = c % 2
    sibling = c + 1 - 2 * odd
    has_up = c + 2 < C
    has_down = c >= 2
    factor = float(HD ** -0.5 * np.log2(np.e))

    def own_copy(kv, head):
        return pltpu.make_async_copy(
            (k_hbm, v_hbm)[kv].at[:, pl.ds(head * HD, HD)], kvg.at[head, c, kv], kv_sem.at[kv, head])

    for head in range(n_kv):
        own_copy(0, head).start()
        own_copy(1, head).start()

    def q_copy(h):
        return pltpu.make_async_copy(
            q_hbm.at[:, pl.ds(pl.multiple_of(h * HD, HD), HD)],
            qs.at[h // group, pl.ds(pl.multiple_of((h % group) * tok, tok), tok), :],
            q_sem.at[h])

    @pl.loop(0, n_kv * group)
    def _(h):
        q_copy(h).start()

    barrier = pltpu.get_barrier_semaphore()
    pl.semaphore_signal(barrier, inc=1, device_id={"context": sibling})

    @pl.when(has_up)
    def _():
        pl.semaphore_signal(barrier, inc=1, device_id={"context": c + 2})

    @pl.when(has_down)
    def _():
        pl.semaphore_signal(barrier, inc=1, device_id={"context": c - 2})

    for d in range(1, N):
        pl.semaphore_signal(barrier, inc=1, device_id={"tensor": lax.rem(t + d, N)})
    pl.semaphore_wait(barrier, N + has_up.astype(jnp.int32) + has_down.astype(jnp.int32))

    def up_copy(head, b):
        return pltpu.make_async_remote_copy(
            src_ref=kvg.at[head, b], dst_ref=kvg.at[head, b],
            send_sem=zs_sem.at[head, b], recv_sem=zr_sem.at[head, b],
            device_id={"context": c + 2})

    def side_copy(head, b):
        return pltpu.make_async_remote_copy(
            src_ref=kvg.at[head, b], dst_ref=kvg.at[head, b],
            send_sem=ss_sem.at[head, b], recv_sem=sr_sem.at[head, b],
            device_id={"context": sibling})

    for head in range(n_kv):
        own_copy(0, head).wait()
        own_copy(1, head).wait()

        @pl.when(has_up)
        def _():
            up_copy(head, c).start()

        @pl.when(odd == 0)
        def _():
            side_copy(head, c).start()

    def w_copy(i):
        cols = pl.ds(pl.multiple_of(i * width, width), width)
        return pltpu.make_async_copy(w_hbm.at[:, cols], wv.at[:, cols], w_sem.at[i])

    @pl.loop(0, N * n_chunk)
    def _(i):
        w_copy(i).start()

    @pl.loop(0, n_kv * group)
    def _(h):
        q_copy(h).wait()

    def attend(head, b0, n_blocks, first):
        n_keys = n_blocks * tok
        key = kvg[head, pl.ds(b0, n_blocks), 0].reshape(n_keys, HD)
        val = kvg[head, pl.ds(b0, n_blocks), 1].reshape(n_keys, HD)
        both = jnp.concatenate([val, jnp.ones_like(val)], axis=1)

        def scores(g):
            return lax.dot_general(qs[head, g * tok:(g + 1) * tok, :], key,
                                   (((1,), (1,)), ((), ())), preferred_element_type=F32)

        s = scores(0)
        for g in range(group):
            ahead = scores(g + 1) if g + 1 < group else None
            here = slice(g * tok, (g + 1) * tok)
            if first:
                r = lax.broadcasted_iota(jnp.int32, s.shape, 0)
                k = lax.broadcasted_iota(jnp.int32, s.shape, 1)
                s = jnp.where(k <= r, s, -1e30)
            parts = [s[:, j * HD:(j + 1) * HD] for j in range(n_keys // HD)]
            m = functools.reduce(jnp.maximum, parts)
            m = jnp.broadcast_to(jnp.max(m, axis=1, keepdims=True), m.shape)
            if not first:
                before = top[head, here, :]
                m = jnp.maximum(before, m)
                shrink = jnp.exp2((before - m) * factor)
            top[head, here, :] = m
            mf = m * factor
            p = jnp.concatenate([jnp.exp2(x * factor - mf).astype(BF16) for x in parts], axis=1)
            pv = jnp.dot(p, both, preferred_element_type=F32)
            if not first:
                pv = acc[head, here, :] * jnp.concatenate([shrink, shrink], axis=1) + pv
            acc[head, here, :] = pv
            s = ahead

    @pl.loop(0, n_kv)
    def _(head):
        attend(head, c, 1, True)

    @pl.when(odd == 1)
    def _():
        @pl.loop(0, n_kv)
        def _(head):
            side_copy(head, sibling).wait_recv()
            attend(head, sibling, 1, False)

    @pl.loop(0, z * n_kv)
    def _(step):
        i = step // n_kv + 1
        head = step % n_kv
        b = c - 2 * i
        up_copy(head, b).wait_recv()

        @pl.when(has_up)
        def _():
            up_copy(head, b).start()

        side_copy(head, b).start()
        side_copy(head, sibling - 2 * i).wait_recv()
        attend(head, 2 * (z - i), 2, False)

    @pl.loop(0, n_kv)
    def _(head):
        for g in range(group):
            a = acc[head, g * tok:(g + 1) * tok, :]
            lanes = pl.ds(pl.multiple_of((head * group + g) * HD, HD), HD)
            att[:, lanes] = (a[:, :HD] / a[:, HD:]).astype(BF16)

    def y_copy(i):
        d = i // n_chunk + 1
        return pltpu.make_async_remote_copy(
            src_ref=sendbuf.at[i], dst_ref=recvbuf.at[i],
            send_sem=ys_sem.at[i], recv_sem=yr_sem.at[i],
            device_id={"tensor": lax.rem(t + d, N)})

    def project(chunk):
        w_copy(chunk).wait()
        cols = pl.ds(pl.multiple_of(chunk * width, width), width)
        return jnp.dot(att[...], wv[:, cols], preferred_element_type=F32).astype(BF16)

    @pl.loop(0, (N - 1) * n_chunk)
    def _(i):
        peer = lax.rem(t + i // n_chunk + 1, N)
        sendbuf[i] = project(peer * n_chunk + i % n_chunk)
        y_copy(i).start()

    @pl.loop(0, n_chunk)
    def _(j):
        total = project(t * n_chunk + j).astype(F32)
        for d in range(N - 1):
            y_copy(d * n_chunk + j).wait_recv()
            total = total + recvbuf[d * n_chunk + j].astype(F32)
        out_ref[:, pl.ds(pl.multiple_of(j * width, width), width)] = total.astype(BF16)

    @pl.loop(0, (N - 1) * n_chunk)
    def _(i):
        y_copy(i).wait_send()

    @pl.when(has_up)
    def _():
        @pl.loop(0, z + 1)
        def _(i):
            for head in range(n_kv):
                up_copy(head, c - 2 * i).wait_send()

    @pl.loop(1 - (odd == 0).astype(jnp.int32), z + 1)
    def _(i):
        for head in range(n_kv):
            side_copy(head, c - 2 * i).wait_send()


def body(C, N, queries, keys, values, out_weight):
    tok, q_width = queries.shape
    kv_width = keys.shape[1]
    n_kv = kv_width // HD
    group = q_width // kv_width
    n_feat, n_out = out_weight.shape
    own_width = n_out // N
    width = min(256, own_width)
    n_chunk = own_width // width
    dims = (C, N, tok, n_kv, group, n_out, width, n_chunk)
    n_send = (N - 1) * n_chunk
    dma = pltpu.SemaphoreType.DMA
    return pl.pallas_call(
        functools.partial(kernel, dims),
        out_shape=jax.ShapeDtypeStruct((tok, own_width), BF16),
        in_specs=[pl.BlockSpec(memory_space=pl.ANY)] * 4,
        out_specs=pl.BlockSpec(memory_space=pltpu.VMEM),
        scratch_shapes=[
            pltpu.VMEM((n_kv, group * tok, HD), BF16),
            pltpu.VMEM((n_kv, C, 2, tok, HD), BF16),
            pltpu.VMEM((n_feat, n_out), BF16),
            pltpu.VMEM((n_kv, group * tok, 2 * HD), F32),
            pltpu.VMEM((n_kv, group * tok, HD), F32),
            pltpu.VMEM((tok, q_width), BF16),
            pltpu.VMEM((n_send, tok, width), BF16),
            pltpu.VMEM((n_send, tok, width), BF16),
            dma((n_kv * group,)),
            dma((2, n_kv)),
            dma((N * n_chunk,)),
            dma((n_kv, C)),
            dma((n_kv, C)),
            dma((n_kv, C)),
            dma((n_kv, C)),
            dma((n_send,)),
            dma((n_send,)),
        ],
        compiler_params=pltpu.CompilerParams(
            collective_id=0, has_side_effects=True, vmem_limit_bytes=67043328
        ),
    )(queries, keys, values, out_weight)


def solution(mesh):
    C, N = mesh.shape["context"], mesh.shape["tensor"]
    return jax.shard_map(
        functools.partial(body, C, N),
        mesh=mesh,
        in_specs=(
            P(("parts", "context"), "tensor"),
            P(("parts", "context"), "tensor"),
            P(("parts", "context"), "tensor"),
            P("tensor", None),
        ),
        out_specs=P(("parts", "context"), "tensor"),
        check_vma=False,
    )
```

```python
import functools

import jax
import jax.numpy as jnp
import numpy as np
from jax import lax
from jax.experimental import pallas as pl
from jax.experimental.pallas import tpu as pltpu
from jax.sharding import PartitionSpec as P

HD = 128
F32 = jnp.float32
BF16 = jnp.bfloat16


def kernel(dims, q_hbm, k_hbm, v_hbm, w_hbm, out_ref,
           qs, kvg, wv, acc, top, att, sendbuf, recvbuf,
           q_sem, kv_sem, w_sem, zs_sem, ss_sem, zr_sem, sr_sem, ys_sem, yr_sem,
           relay1, relay2, r1r_sem, r1s_sem, r2r_sem, r2s_sem):
    C, N, tok, n_kv, group, n_out, width, n_chunk = dims
    c = lax.axis_index("context")
    t = lax.axis_index("tensor")
    z = c // 2
    odd = c % 2
    sibling = c + 1 - 2 * odd
    has_up = c + 2 < C
    has_down = c >= 2
    n_send = (N - 1) * n_chunk
    half = width // 2
    is_last = (c >= C - 2) & (C >= 6)
    is_relay = (c < 2) & (C >= 6)
    far = jnp.where(c < 2, c + C - 2, odd)
    factor = float(HD ** -0.5 * np.log2(np.e))

    def own_copy(kv, head):
        return pltpu.make_async_copy(
            (k_hbm, v_hbm)[kv].at[:, pl.ds(head * HD, HD)], kvg.at[head, c, kv], kv_sem.at[kv, head])

    for head in range(n_kv):
        own_copy(0, head).start()
        own_copy(1, head).start()

    def q_copy(h):
        return pltpu.make_async_copy(
            q_hbm.at[:, pl.ds(pl.multiple_of(h * HD, HD), HD)],
            qs.at[h // group, pl.ds(pl.multiple_of((h % group) * tok, tok), tok), :],
            q_sem.at[h])

    @pl.loop(0, n_kv * group)
    def _(h):
        q_copy(h).start()

    barrier = pltpu.get_barrier_semaphore()
    pl.semaphore_signal(barrier, inc=1, device_id={"context": sibling})

    @pl.when(has_up)
    def _():
        pl.semaphore_signal(barrier, inc=1, device_id={"context": c + 2})

    @pl.when(has_down)
    def _():
        pl.semaphore_signal(barrier, inc=1, device_id={"context": c - 2})

    for d in range(1, N):
        pl.semaphore_signal(barrier, inc=1, device_id={"tensor": lax.rem(t + d, N)})

    @pl.when(is_last | is_relay)
    def _():
        pl.semaphore_signal(barrier, inc=1, device_id={"context": far})

    pl.semaphore_wait(barrier, N + (is_last | is_relay).astype(jnp.int32) + has_up.astype(jnp.int32) + has_down.astype(jnp.int32))

    def up_copy(head, b):
        return pltpu.make_async_remote_copy(
            src_ref=kvg.at[head, b], dst_ref=kvg.at[head, b],
            send_sem=zs_sem.at[head, b], recv_sem=zr_sem.at[head, b],
            device_id={"context": c + 2})

    def side_copy(head, b):
        return pltpu.make_async_remote_copy(
            src_ref=kvg.at[head, b], dst_ref=kvg.at[head, b],
            send_sem=ss_sem.at[head, b], recv_sem=sr_sem.at[head, b],
            device_id={"context": sibling})

    for head in range(n_kv):
        own_copy(0, head).wait()
        own_copy(1, head).wait()

        @pl.when(has_up)
        def _():
            up_copy(head, c).start()

        @pl.when(odd == 0)
        def _():
            side_copy(head, c).start()

    def w_copy(i):
        cols = pl.ds(pl.multiple_of(i * width, width), width)
        return pltpu.make_async_copy(w_hbm.at[:, cols], wv.at[:, cols], w_sem.at[i])

    @pl.loop(0, N * n_chunk)
    def _(i):
        w_copy(i).start()

    @pl.loop(0, n_kv * group)
    def _(h):
        q_copy(h).wait()

    def attend(head, b0, n_blocks, first):
        n_keys = n_blocks * tok
        key = kvg[head, pl.ds(b0, n_blocks), 0].reshape(n_keys, HD)
        val = kvg[head, pl.ds(b0, n_blocks), 1].reshape(n_keys, HD)
        both = jnp.concatenate([val, jnp.ones_like(val)], axis=1)

        def scores(g):
            return lax.dot_general(qs[head, g * tok:(g + 1) * tok, :], key,
                                   (((1,), (1,)), ((), ())), preferred_element_type=F32)

        s = scores(0)
        for g in range(group):
            ahead = scores(g + 1) if g + 1 < group else None
            here = slice(g * tok, (g + 1) * tok)
            if first:
                r = lax.broadcasted_iota(jnp.int32, s.shape, 0)
                k = lax.broadcasted_iota(jnp.int32, s.shape, 1)
                s = jnp.where(k <= r, s, -1e30)
            parts = [s[:, j * HD:(j + 1) * HD] for j in range(n_keys // HD)]
            m = functools.reduce(jnp.maximum, parts)
            m = jnp.broadcast_to(jnp.max(m, axis=1, keepdims=True), m.shape)
            if not first:
                before = top[head, here, :]
                m = jnp.maximum(before, m)
                shrink = jnp.exp2((before - m) * factor)
            top[head, here, :] = m
            mf = m * factor
            p = jnp.concatenate([jnp.exp2(x * factor - mf).astype(BF16) for x in parts], axis=1)
            pv = jnp.dot(p, both, preferred_element_type=F32)
            if not first:
                pv = acc[head, here, :] * jnp.concatenate([shrink, shrink], axis=1) + pv
            acc[head, here, :] = pv
            s = ahead

    @pl.loop(0, n_kv)
    def _(head):
        attend(head, c, 1, True)

    @pl.when(odd == 1)
    def _():
        @pl.loop(0, n_kv)
        def _(head):
            side_copy(head, sibling).wait_recv()
            attend(head, sibling, 1, False)

    @pl.loop(0, z * n_kv)
    def _(step):
        i = step // n_kv + 1
        head = step % n_kv
        b = c - 2 * i
        up_copy(head, b).wait_recv()

        @pl.when(has_up)
        def _():
            up_copy(head, b).start()

        side_copy(head, b).start()
        side_copy(head, sibling - 2 * i).wait_recv()
        attend(head, 2 * (z - i), 2, False)

    @pl.loop(0, n_kv)
    def _(head):
        for g in range(group):
            a = acc[head, g * tok:(g + 1) * tok, :]
            lanes = pl.ds(pl.multiple_of((head * group + g) * HD, HD), HD)
            att[:, lanes] = (a[:, :HD] / a[:, HD:]).astype(BF16)

    def y_peer(i):
        return {"tensor": lax.rem(t + i // n_chunk + 1, N)}

    def slot(i):
        return i // 8 * 3 + i % 8 // 2

    def y_copy(i, h):
        return pltpu.make_async_remote_copy(
            src_ref=sendbuf.at[i, h], dst_ref=recvbuf.at[i, h],
            send_sem=ys_sem.at[i, h], recv_sem=yr_sem.at[i, h], device_id=y_peer(i))

    def down_copy(i, h):
        return pltpu.make_async_remote_copy(
            src_ref=sendbuf.at[i, h], dst_ref=relay1.at[slot(i), h],
            send_sem=ys_sem.at[i, h], recv_sem=r1r_sem.at[slot(i), h], device_id={"context": far})

    def cross_copy(i, h):
        return pltpu.make_async_remote_copy(
            src_ref=relay1.at[slot(i), h], dst_ref=relay2.at[slot(i), h],
            send_sem=r1s_sem.at[slot(i), h], recv_sem=r2r_sem.at[slot(i), h], device_id=y_peer(i))

    def back_copy(i, h):
        return pltpu.make_async_remote_copy(
            src_ref=relay2.at[slot(i), h], dst_ref=recvbuf.at[i, h],
            send_sem=r2s_sem.at[slot(i), h], recv_sem=yr_sem.at[i, h], device_id={"context": far})

    def project(chunk):
        w_copy(chunk).wait()
        cols = pl.ds(pl.multiple_of(chunk * width, width), width)
        return jnp.dot(att[...], wv[:, cols], preferred_element_type=F32).astype(BF16)

    @pl.loop(0, n_send)
    def _(i):
        peer = lax.rem(t + i // n_chunk + 1, N)
        term = project(peer * n_chunk + i % n_chunk)
        detour = is_last & (i % 8 < 5) & (i % 2 == 0)
        for h in range(2):
            sendbuf[i, h] = term[:, h * half:(h + 1) * half]

        @pl.when(detour)
        def _():
            for h in range(2):
                down_copy(i, h).start()

        @pl.when(jnp.logical_not(detour))
        def _():
            for h in range(2):
                y_copy(i, h).start()

    def order(jj):
        return jnp.where(jj < n_chunk // 2, 2 * jj + 1, 2 * (jj - n_chunk // 2))

    @pl.loop(0, n_chunk)
    def _(jj):
        j = order(jj)
        total = project(t * n_chunk + j).astype(F32)
        for h in range(2):
            part = total[:, h * half:(h + 1) * half]
            for d in range(N - 1):
                y_copy(d * n_chunk + j, h).wait_recv()
                part = part + recvbuf[d * n_chunk + j, h].astype(F32)
            out_ref[:, pl.ds(pl.multiple_of(j * width + h * half, half), half)] = part.astype(BF16)

    @pl.when(is_relay)
    def _():
        subs = [(i, h) for i in range(n_send) if i % 8 in (0, 2, 4) for h in range(2)]
        for n in range(len(subs) + 2):
            if n < len(subs):
                down_copy(*subs[n]).wait_recv()
                cross_copy(*subs[n]).start()
            if n >= 2:
                cross_copy(*subs[n - 2]).wait_recv()
                back_copy(*subs[n - 2]).start()
        for sub in subs:
            cross_copy(*sub).wait_send()
            back_copy(*sub).wait_send()

    @pl.loop(0, n_send)
    def _(i):
        for h in range(2):
            y_copy(i, h).wait_send()

    @pl.when(has_up)
    def _():
        @pl.loop(0, z + 1)
        def _(i):
            for head in range(n_kv):
                up_copy(head, c - 2 * i).wait_send()

    @pl.loop(1 - (odd == 0).astype(jnp.int32), z + 1)
    def _(i):
        for head in range(n_kv):
            side_copy(head, c - 2 * i).wait_send()


def body(C, N, queries, keys, values, out_weight):
    tok, q_width = queries.shape
    kv_width = keys.shape[1]
    n_kv = kv_width // HD
    group = q_width // kv_width
    n_feat, n_out = out_weight.shape
    own_width = n_out // N
    width = min(256, own_width)
    n_chunk = own_width // width
    dims = (C, N, tok, n_kv, group, n_out, width, n_chunk)
    n_send = (N - 1) * n_chunk
    n_det = (n_send + 7) // 8 * 3
    dma = pltpu.SemaphoreType.DMA
    return pl.pallas_call(
        functools.partial(kernel, dims),
        out_shape=jax.ShapeDtypeStruct((tok, own_width), BF16),
        in_specs=[pl.BlockSpec(memory_space=pl.ANY)] * 4,
        out_specs=pl.BlockSpec(memory_space=pltpu.VMEM),
        scratch_shapes=[
            pltpu.VMEM((n_kv, group * tok, HD), BF16),
            pltpu.VMEM((n_kv, C, 2, tok, HD), BF16),
            pltpu.VMEM((n_feat, n_out), BF16),
            pltpu.VMEM((n_kv, group * tok, 2 * HD), F32),
            pltpu.VMEM((n_kv, group * tok, HD), F32),
            pltpu.VMEM((tok, q_width), BF16),
            pltpu.VMEM((n_send, 2, tok, width // 2), BF16),
            pltpu.VMEM((n_send, 2, tok, width // 2), BF16),
            dma((n_kv * group,)),
            dma((2, n_kv)),
            dma((N * n_chunk,)),
            dma((n_kv, C)),
            dma((n_kv, C)),
            dma((n_kv, C)),
            dma((n_kv, C)),
            dma((n_send, 2)),
            dma((n_send, 2)),
            pltpu.VMEM((n_det, 2, tok, width // 2), BF16),
            pltpu.VMEM((n_det, 2, tok, width // 2), BF16),
            dma((n_det, 2)),
            dma((n_det, 2)),
            dma((n_det, 2)),
            dma((n_det, 2)),
        ],
        compiler_params=pltpu.CompilerParams(
            collective_id=0, has_side_effects=True, vmem_limit_bytes=67043328
        ),
    )(queries, keys, values, out_weight)


def solution(mesh):
    C, N = mesh.shape["context"], mesh.shape["tensor"]
    return jax.shard_map(
        functools.partial(body, C, N),
        mesh=mesh,
        in_specs=(
            P(("parts", "context"), "tensor"),
            P(("parts", "context"), "tensor"),
            P(("parts", "context"), "tensor"),
            P("tensor", None),
        ),
        out_specs=P(("parts", "context"), "tensor"),
        check_vma=False,
    )
```

```python
import functools

import jax
import jax.numpy as jnp
import numpy as np
from jax import lax
from jax.experimental import pallas as pl
from jax.experimental.pallas import tpu as pltpu
from jax.sharding import PartitionSpec as P

HD = 128
F32 = jnp.float32
BF16 = jnp.bfloat16


def kernel(dims, q_hbm, k_hbm, v_hbm, w_hbm, out_ref,
           qs, kvg, wv, acc, top, att, sendbuf, recvbuf,
           q_sem, kv_sem, w_sem, zs_sem, ss_sem, zr_sem, sr_sem, ys_sem, yr_sem,
           relay1, relay2, r1r_sem, r1s_sem, r2r_sem, r2s_sem):
    C, N, tok, n_kv, group, n_out, width, n_chunk = dims
    c = lax.axis_index("context")
    t = lax.axis_index("tensor")
    z = c // 2
    odd = c % 2
    sibling = c + 1 - 2 * odd
    has_up = c + 2 < C
    has_down = c >= 2
    n_send = (N - 1) * n_chunk
    half = width // 2
    is_last = (c >= C - 2) & (C >= 6)
    is_relay = (c < 2) & (C >= 6)
    far = jnp.where(c < 2, c + C - 2, odd)
    factor = float(HD ** -0.5 * np.log2(np.e))

    def own_copy(kv, head):
        return pltpu.make_async_copy(
            (k_hbm, v_hbm)[kv].at[:, pl.ds(head * HD, HD)], kvg.at[head, c, kv], kv_sem.at[kv, head])

    for head in range(n_kv):
        own_copy(0, head).start()
        own_copy(1, head).start()

    def q_copy(h):
        return pltpu.make_async_copy(
            q_hbm.at[:, pl.ds(pl.multiple_of(h * HD, HD), HD)],
            qs.at[h // group, pl.ds(pl.multiple_of((h % group) * tok, tok), tok), :],
            q_sem.at[h])

    @pl.loop(0, n_kv * group)
    def _(h):
        q_copy(h).start()

    barrier = pltpu.get_barrier_semaphore()
    pl.semaphore_signal(barrier, inc=1, device_id={"context": sibling})

    @pl.when(has_up)
    def _():
        pl.semaphore_signal(barrier, inc=1, device_id={"context": c + 2})

    @pl.when(has_down)
    def _():
        pl.semaphore_signal(barrier, inc=1, device_id={"context": c - 2})

    for d in range(1, N):
        pl.semaphore_signal(barrier, inc=1, device_id={"tensor": lax.rem(t + d, N)})

    @pl.when(is_last | is_relay)
    def _():
        pl.semaphore_signal(barrier, inc=1, device_id={"context": far})

    pl.semaphore_wait(barrier, N + (is_last | is_relay).astype(jnp.int32) + has_up.astype(jnp.int32) + has_down.astype(jnp.int32))

    def up_copy(head, b):
        return pltpu.make_async_remote_copy(
            src_ref=kvg.at[head, b], dst_ref=kvg.at[head, b],
            send_sem=zs_sem.at[head, b], recv_sem=zr_sem.at[head, b],
            device_id={"context": c + 2})

    def side_copy(head, b):
        return pltpu.make_async_remote_copy(
            src_ref=kvg.at[head, b], dst_ref=kvg.at[head, b],
            send_sem=ss_sem.at[head, b], recv_sem=sr_sem.at[head, b],
            device_id={"context": sibling})

    for head in range(n_kv):
        own_copy(0, head).wait()
        own_copy(1, head).wait()

        @pl.when(has_up)
        def _():
            up_copy(head, c).start()

        @pl.when(odd == 0)
        def _():
            side_copy(head, c).start()

    def w_copy(i):
        cols = pl.ds(pl.multiple_of(i * width, width), width)
        return pltpu.make_async_copy(w_hbm.at[:, cols], wv.at[:, cols], w_sem.at[i])

    @pl.loop(0, N * n_chunk)
    def _(i):
        w_copy(i).start()

    @pl.loop(0, n_kv * group)
    def _(h):
        q_copy(h).wait()

    def attend(head, b0, n_blocks, first):
        n_keys = n_blocks * tok
        key = kvg[head, pl.ds(b0, n_blocks), 0].reshape(n_keys, HD)
        val = kvg[head, pl.ds(b0, n_blocks), 1].reshape(n_keys, HD)
        both = jnp.concatenate([val, jnp.ones_like(val)], axis=1)

        def scores(g):
            return lax.dot_general(qs[head, g * tok:(g + 1) * tok, :], key,
                                   (((1,), (1,)), ((), ())), preferred_element_type=F32)

        s = scores(0)
        for g in range(group):
            ahead = scores(g + 1) if g + 1 < group else None
            here = slice(g * tok, (g + 1) * tok)
            if first:
                r = lax.broadcasted_iota(jnp.int32, s.shape, 0)
                k = lax.broadcasted_iota(jnp.int32, s.shape, 1)
                s = jnp.where(k <= r, s, -1e30)
            parts = [s[:, j * HD:(j + 1) * HD] for j in range(n_keys // HD)]
            m = functools.reduce(jnp.maximum, parts)
            m = jnp.broadcast_to(jnp.max(m, axis=1, keepdims=True), m.shape)
            if not first:
                before = top[head, here, :]
                m = jnp.maximum(before, m)
                shrink = jnp.exp2((before - m) * factor)
            top[head, here, :] = m
            mf = m * factor
            p = jnp.concatenate([jnp.exp2(x * factor - mf).astype(BF16) for x in parts], axis=1)
            pv = jnp.dot(p, both, preferred_element_type=F32)
            if not first:
                pv = acc[head, here, :] * jnp.concatenate([shrink, shrink], axis=1) + pv
            acc[head, here, :] = pv
            s = ahead

    @pl.loop(0, n_kv)
    def _(head):
        attend(head, c, 1, True)

    @pl.when(odd == 1)
    def _():
        @pl.loop(0, n_kv)
        def _(head):
            side_copy(head, sibling).wait_recv()
            attend(head, sibling, 1, False)

    @pl.loop(0, z * n_kv)
    def _(step):
        i = step // n_kv + 1
        head = step % n_kv
        b = c - 2 * i
        up_copy(head, b).wait_recv()

        @pl.when(has_up)
        def _():
            up_copy(head, b).start()

        side_copy(head, b).start()
        side_copy(head, sibling - 2 * i).wait_recv()
        attend(head, 2 * (z - i), 2, False)

    @pl.loop(0, n_kv)
    def _(head):
        for g in range(group):
            a = acc[head, g * tok:(g + 1) * tok, :]
            lanes = pl.ds(pl.multiple_of((head * group + g) * HD, HD), HD)
            att[:, lanes] = (a[:, :HD] / a[:, HD:]).astype(BF16)

    def y_peer(i):
        return {"tensor": lax.rem(t + i // n_chunk + 1, N)}

    def slot(i):
        return i // 8 * 3 + i % 8 // 2

    def y_copy(i, h):
        return pltpu.make_async_remote_copy(
            src_ref=sendbuf.at[i, h], dst_ref=recvbuf.at[i, h],
            send_sem=ys_sem.at[i, h], recv_sem=yr_sem.at[i, h], device_id=y_peer(i))

    def down_copy(i, h):
        return pltpu.make_async_remote_copy(
            src_ref=sendbuf.at[i, h], dst_ref=relay1.at[slot(i), h],
            send_sem=ys_sem.at[i, h], recv_sem=r1r_sem.at[slot(i), h], device_id={"context": far})

    def cross_copy(i, h):
        return pltpu.make_async_remote_copy(
            src_ref=relay1.at[slot(i), h], dst_ref=relay2.at[slot(i), h],
            send_sem=r1s_sem.at[slot(i), h], recv_sem=r2r_sem.at[slot(i), h], device_id=y_peer(i))

    def back_copy(i, h):
        return pltpu.make_async_remote_copy(
            src_ref=relay2.at[slot(i), h], dst_ref=recvbuf.at[i, h],
            send_sem=r2s_sem.at[slot(i), h], recv_sem=yr_sem.at[i, h], device_id={"context": far})

    def project(chunk):
        w_copy(chunk).wait()
        cols = pl.ds(pl.multiple_of(chunk * width, width), width)
        return jnp.dot(att[...], wv[:, cols], preferred_element_type=F32).astype(BF16)

    @pl.loop(0, n_send)
    def _(i):
        peer = lax.rem(t + i // n_chunk + 1, N)
        term = project(peer * n_chunk + i % n_chunk)
        detour = is_last & (i % 8 < 5) & (i % 2 == 0)
        for h in range(2):
            sendbuf[i, h] = term[:, h * half:(h + 1) * half]

        @pl.when(detour)
        def _():
            for h in range(2):
                down_copy(i, h).start()

        @pl.when(jnp.logical_not(detour))
        def _():
            for h in range(2):
                y_copy(i, h).start()

    @pl.loop(0, n_chunk)
    def _(j):
        out_ref[:, pl.ds(pl.multiple_of(j * width, width), width)] = project(t * n_chunk + j)

    def order(jj):
        return jnp.where(jj < n_chunk // 2, 2 * jj + 1, 2 * (jj - n_chunk // 2))

    @pl.loop(0, n_chunk)
    def _(jj):
        j = order(jj)
        for h in range(2):
            cols = pl.ds(pl.multiple_of(j * width + h * half, half), half)
            part = out_ref[:, cols].astype(F32)
            for d in range(N - 1):
                y_copy(d * n_chunk + j, h).wait_recv()
                part = part + recvbuf[d * n_chunk + j, h].astype(F32)
            out_ref[:, cols] = part.astype(BF16)

    @pl.when(is_relay)
    def _():
        subs = [(i, h) for i in range(n_send) if i % 8 in (0, 2, 4) for h in range(2)]
        for n in range(len(subs) + 2):
            if n < len(subs):
                down_copy(*subs[n]).wait_recv()
                cross_copy(*subs[n]).start()
            if n >= 2:
                cross_copy(*subs[n - 2]).wait_recv()
                back_copy(*subs[n - 2]).start()
        for sub in subs:
            cross_copy(*sub).wait_send()
            back_copy(*sub).wait_send()

    @pl.loop(0, n_send)
    def _(i):
        for h in range(2):
            y_copy(i, h).wait_send()

    @pl.when(has_up)
    def _():
        @pl.loop(0, z + 1)
        def _(i):
            for head in range(n_kv):
                up_copy(head, c - 2 * i).wait_send()

    @pl.loop(1 - (odd == 0).astype(jnp.int32), z + 1)
    def _(i):
        for head in range(n_kv):
            side_copy(head, c - 2 * i).wait_send()


def body(C, N, queries, keys, values, out_weight):
    tok, q_width = queries.shape
    kv_width = keys.shape[1]
    n_kv = kv_width // HD
    group = q_width // kv_width
    n_feat, n_out = out_weight.shape
    own_width = n_out // N
    width = min(256, own_width)
    n_chunk = own_width // width
    dims = (C, N, tok, n_kv, group, n_out, width, n_chunk)
    n_send = (N - 1) * n_chunk
    n_det = (n_send + 7) // 8 * 3
    dma = pltpu.SemaphoreType.DMA
    return pl.pallas_call(
        functools.partial(kernel, dims),
        out_shape=jax.ShapeDtypeStruct((tok, own_width), BF16),
        in_specs=[pl.BlockSpec(memory_space=pl.ANY)] * 4,
        out_specs=pl.BlockSpec(memory_space=pltpu.VMEM),
        scratch_shapes=[
            pltpu.VMEM((n_kv, group * tok, HD), BF16),
            pltpu.VMEM((n_kv, C, 2, tok, HD), BF16),
            pltpu.VMEM((n_feat, n_out), BF16),
            pltpu.VMEM((n_kv, group * tok, 2 * HD), F32),
            pltpu.VMEM((n_kv, group * tok, HD), F32),
            pltpu.VMEM((tok, q_width), BF16),
            pltpu.VMEM((n_send, 2, tok, width // 2), BF16),
            pltpu.VMEM((n_send, 2, tok, width // 2), BF16),
            dma((n_kv * group,)),
            dma((2, n_kv)),
            dma((N * n_chunk,)),
            dma((n_kv, C)),
            dma((n_kv, C)),
            dma((n_kv, C)),
            dma((n_kv, C)),
            dma((n_send, 2)),
            dma((n_send, 2)),
            pltpu.VMEM((n_det, 2, tok, width // 2), BF16),
            pltpu.VMEM((n_det, 2, tok, width // 2), BF16),
            dma((n_det, 2)),
            dma((n_det, 2)),
            dma((n_det, 2)),
            dma((n_det, 2)),
        ],
        compiler_params=pltpu.CompilerParams(
            collective_id=0, has_side_effects=True, vmem_limit_bytes=67043328
        ),
    )(queries, keys, values, out_weight)


def solution(mesh):
    C, N = mesh.shape["context"], mesh.shape["tensor"]
    return jax.shard_map(
        functools.partial(body, C, N),
        mesh=mesh,
        in_specs=(
            P(("parts", "context"), "tensor"),
            P(("parts", "context"), "tensor"),
            P(("parts", "context"), "tensor"),
            P("tensor", None),
        ),
        out_specs=P(("parts", "context"), "tensor"),
        check_vma=False,
    )
```

```python
import functools

import jax
import jax.numpy as jnp
import numpy as np
from jax import lax
from jax.experimental import pallas as pl
from jax.experimental.pallas import tpu as pltpu
from jax.sharding import PartitionSpec as P

HD = 128
F32 = jnp.float32
BF16 = jnp.bfloat16


def kernel(dims, q_hbm, k_hbm, v_hbm, w_hbm, out_ref,
           qs, kvg, wv, acc, top, att, sendbuf, recvbuf,
           q_sem, kv_sem, w_sem, zs_sem, ss_sem, zr_sem, sr_sem, ys_sem, yr_sem,
           relay1, relay2, r1r_sem, r1s_sem, r2r_sem, r2s_sem):
    C, N, tok, n_kv, group, n_out, width, n_chunk = dims
    c = lax.axis_index("context")
    t = lax.axis_index("tensor")
    z = c // 2
    odd = c % 2
    sibling = c + 1 - 2 * odd
    has_up = c + 2 < C
    has_down = c >= 2
    n_send = (N - 1) * n_chunk
    half = width // 2
    is_last = (c >= C - 2) & (C >= 6)
    is_relay = (c < 2) & (C >= 6)
    far = jnp.where(c < 2, c + C - 2, odd)
    factor = float(HD ** -0.5 * np.log2(np.e))

    def own_copy(kv, head):
        return pltpu.make_async_copy(
            (k_hbm, v_hbm)[kv].at[:, pl.ds(head * HD, HD)], kvg.at[head, c, kv], kv_sem.at[kv, head])

    for head in range(n_kv):
        own_copy(0, head).start()
        own_copy(1, head).start()

    def q_copy(h):
        return pltpu.make_async_copy(
            q_hbm.at[:, pl.ds(pl.multiple_of(h * HD, HD), HD)],
            qs.at[h // group, pl.ds(pl.multiple_of((h % group) * tok, tok), tok), :],
            q_sem.at[h])

    @pl.loop(0, n_kv * group)
    def _(h):
        q_copy(h).start()

    barrier = pltpu.get_barrier_semaphore()
    pl.semaphore_signal(barrier, inc=1, device_id={"context": sibling})

    @pl.when(has_up)
    def _():
        pl.semaphore_signal(barrier, inc=1, device_id={"context": c + 2})

    @pl.when(has_down)
    def _():
        pl.semaphore_signal(barrier, inc=1, device_id={"context": c - 2})

    for d in range(1, N):
        pl.semaphore_signal(barrier, inc=1, device_id={"tensor": lax.rem(t + d, N)})

    @pl.when(is_last | is_relay)
    def _():
        pl.semaphore_signal(barrier, inc=1, device_id={"context": far})

    pl.semaphore_wait(barrier, N + (is_last | is_relay).astype(jnp.int32) + has_up.astype(jnp.int32) + has_down.astype(jnp.int32))

    def up_copy(head, b):
        return pltpu.make_async_remote_copy(
            src_ref=kvg.at[head, b], dst_ref=kvg.at[head, b],
            send_sem=zs_sem.at[head, b], recv_sem=zr_sem.at[head, b],
            device_id={"context": c + 2})

    def side_copy(head, b):
        return pltpu.make_async_remote_copy(
            src_ref=kvg.at[head, b], dst_ref=kvg.at[head, b],
            send_sem=ss_sem.at[head, b], recv_sem=sr_sem.at[head, b],
            device_id={"context": sibling})

    for head in range(n_kv):
        own_copy(0, head).wait()
        own_copy(1, head).wait()

        @pl.when(has_up)
        def _():
            up_copy(head, c).start()

        @pl.when(odd == 0)
        def _():
            side_copy(head, c).start()

    def w_copy(i):
        cols = pl.ds(pl.multiple_of(i * width, width), width)
        return pltpu.make_async_copy(w_hbm.at[:, cols], wv.at[:, cols], w_sem.at[i])

    @pl.loop(0, N * n_chunk)
    def _(i):
        w_copy(i).start()

    @pl.loop(0, n_kv * group)
    def _(h):
        q_copy(h).wait()

    def attend(head, b0, n_blocks, first):
        n_keys = n_blocks * tok
        key = kvg[head, pl.ds(b0, n_blocks), 0].reshape(n_keys, HD)
        val = kvg[head, pl.ds(b0, n_blocks), 1].reshape(n_keys, HD)
        both = jnp.concatenate([val, jnp.ones_like(val)], axis=1)

        def scores(g):
            return lax.dot_general(qs[head, g * tok:(g + 1) * tok, :], key,
                                   (((1,), (1,)), ((), ())), preferred_element_type=F32)

        s = scores(0)
        for g in range(group):
            ahead = scores(g + 1) if g + 1 < group else None
            here = slice(g * tok, (g + 1) * tok)
            if first:
                r = lax.broadcasted_iota(jnp.int32, s.shape, 0)
                k = lax.broadcasted_iota(jnp.int32, s.shape, 1)
                s = jnp.where(k <= r, s, -1e30)
            parts = [s[:, j * HD:(j + 1) * HD] for j in range(n_keys // HD)]
            m = functools.reduce(jnp.maximum, parts)
            m = jnp.broadcast_to(jnp.max(m, axis=1, keepdims=True), m.shape)
            if not first:
                before = top[head, here, :]
                m = jnp.maximum(before, m)
                shrink = jnp.exp2((before - m) * factor)
            top[head, here, :] = m
            mf = m * factor
            p = jnp.concatenate([jnp.exp2(x * factor - mf).astype(BF16) for x in parts], axis=1)
            pv = jnp.dot(p, both, preferred_element_type=F32)
            if not first:
                pv = acc[head, here, :] * jnp.concatenate([shrink, shrink], axis=1) + pv
            acc[head, here, :] = pv
            s = ahead

    @pl.loop(0, n_kv)
    def _(head):
        attend(head, c, 1, True)

    @pl.when(odd == 1)
    def _():
        @pl.loop(0, n_kv)
        def _(head):
            side_copy(head, sibling).wait_recv()
            attend(head, sibling, 1, False)

    @pl.loop(0, z * n_kv)
    def _(step):
        i = step // n_kv + 1
        head = step % n_kv
        b = c - 2 * i
        up_copy(head, b).wait_recv()

        @pl.when(has_up)
        def _():
            up_copy(head, b).start()

        side_copy(head, b).start()
        side_copy(head, sibling - 2 * i).wait_recv()
        attend(head, 2 * (z - i), 2, False)

    @pl.loop(0, n_kv)
    def _(head):
        for g in range(group):
            a = acc[head, g * tok:(g + 1) * tok, :]
            lanes = pl.ds(pl.multiple_of((head * group + g) * HD, HD), HD)
            att[:, lanes] = (a[:, :HD] / a[:, HD:]).astype(BF16)

    def y_peer(i):
        return {"tensor": lax.rem(t + i // n_chunk + 1, N)}

    def slot(i):
        return i // 8 * 3 + i % 8 // 2

    def y_copy(i, h):
        return pltpu.make_async_remote_copy(
            src_ref=sendbuf.at[i, h], dst_ref=recvbuf.at[i, h],
            send_sem=ys_sem.at[i, h], recv_sem=yr_sem.at[i, h], device_id=y_peer(i))

    def down_copy(i, h):
        return pltpu.make_async_remote_copy(
            src_ref=sendbuf.at[i, h], dst_ref=relay1.at[slot(i), h],
            send_sem=ys_sem.at[i, h], recv_sem=r1r_sem.at[slot(i), h], device_id={"context": far})

    def cross_copy(i, h):
        return pltpu.make_async_remote_copy(
            src_ref=relay1.at[slot(i), h], dst_ref=relay2.at[slot(i), h],
            send_sem=r1s_sem.at[slot(i), h], recv_sem=r2r_sem.at[slot(i), h], device_id=y_peer(i))

    def back_copy(i, h):
        return pltpu.make_async_remote_copy(
            src_ref=relay2.at[slot(i), h], dst_ref=recvbuf.at[i, h],
            send_sem=r2s_sem.at[slot(i), h], recv_sem=yr_sem.at[i, h], device_id={"context": far})

    def project(chunk):
        w_copy(chunk).wait()
        cols = pl.ds(pl.multiple_of(chunk * width, width), width)
        return jnp.dot(att[...], wv[:, cols], preferred_element_type=F32).astype(BF16)

    @pl.loop(0, n_send)
    def _(i):
        peer = lax.rem(t + i // n_chunk + 1, N)
        term = project(peer * n_chunk + i % n_chunk)
        detour = is_last & (i % 8 < 3) & (i % 2 == 0)
        for h in range(2):
            sendbuf[i, h] = term[:, h * half:(h + 1) * half]

        @pl.when(detour)
        def _():
            for h in range(2):
                down_copy(i, h).start()

        @pl.when(jnp.logical_not(detour))
        def _():
            for h in range(2):
                y_copy(i, h).start()

    @pl.loop(0, n_chunk)
    def _(j):
        out_ref[:, pl.ds(pl.multiple_of(j * width, width), width)] = project(t * n_chunk + j)

    def order(jj):
        return jnp.where(jj < n_chunk // 2, 2 * jj + 1, 2 * (jj - n_chunk // 2))

    @pl.loop(0, n_chunk)
    def _(jj):
        j = order(jj)
        for h in range(2):
            cols = pl.ds(pl.multiple_of(j * width + h * half, half), half)
            part = out_ref[:, cols].astype(F32)
            for d in range(N - 1):
                y_copy(d * n_chunk + j, h).wait_recv()
                part = part + recvbuf[d * n_chunk + j, h].astype(F32)
            out_ref[:, cols] = part.astype(BF16)

    @pl.when(is_relay)
    def _():
        subs = [(i, h) for i in range(n_send) if i % 8 in (0, 2) for h in range(2)]
        for n in range(len(subs) + 2):
            if n < len(subs):
                down_copy(*subs[n]).wait_recv()
                cross_copy(*subs[n]).start()
            if n >= 2:
                cross_copy(*subs[n - 2]).wait_recv()
                back_copy(*subs[n - 2]).start()
        for sub in subs:
            cross_copy(*sub).wait_send()
            back_copy(*sub).wait_send()

    @pl.loop(0, n_send)
    def _(i):
        for h in range(2):
            y_copy(i, h).wait_send()

    @pl.when(has_up)
    def _():
        @pl.loop(0, z + 1)
        def _(i):
            for head in range(n_kv):
                up_copy(head, c - 2 * i).wait_send()

    @pl.loop(1 - (odd == 0).astype(jnp.int32), z + 1)
    def _(i):
        for head in range(n_kv):
            side_copy(head, c - 2 * i).wait_send()


def body(C, N, queries, keys, values, out_weight):
    tok, q_width = queries.shape
    kv_width = keys.shape[1]
    n_kv = kv_width // HD
    group = q_width // kv_width
    n_feat, n_out = out_weight.shape
    own_width = n_out // N
    width = min(256, own_width)
    n_chunk = own_width // width
    dims = (C, N, tok, n_kv, group, n_out, width, n_chunk)
    n_send = (N - 1) * n_chunk
    n_det = (n_send + 7) // 8 * 3
    dma = pltpu.SemaphoreType.DMA
    return pl.pallas_call(
        functools.partial(kernel, dims),
        out_shape=jax.ShapeDtypeStruct((tok, own_width), BF16),
        in_specs=[pl.BlockSpec(memory_space=pl.ANY)] * 4,
        out_specs=pl.BlockSpec(memory_space=pltpu.VMEM),
        scratch_shapes=[
            pltpu.VMEM((n_kv, group * tok, HD), BF16),
            pltpu.VMEM((n_kv, C, 2, tok, HD), BF16),
            pltpu.VMEM((n_feat, n_out), BF16),
            pltpu.VMEM((n_kv, group * tok, 2 * HD), F32),
            pltpu.VMEM((n_kv, group * tok, HD), F32),
            pltpu.VMEM((tok, q_width), BF16),
            pltpu.VMEM((n_send, 2, tok, width // 2), BF16),
            pltpu.VMEM((n_send, 2, tok, width // 2), BF16),
            dma((n_kv * group,)),
            dma((2, n_kv)),
            dma((N * n_chunk,)),
            dma((n_kv, C)),
            dma((n_kv, C)),
            dma((n_kv, C)),
            dma((n_kv, C)),
            dma((n_send, 2)),
            dma((n_send, 2)),
            pltpu.VMEM((n_det, 2, tok, width // 2), BF16),
            pltpu.VMEM((n_det, 2, tok, width // 2), BF16),
            dma((n_det, 2)),
            dma((n_det, 2)),
            dma((n_det, 2)),
            dma((n_det, 2)),
        ],
        compiler_params=pltpu.CompilerParams(
            collective_id=0, has_side_effects=True, vmem_limit_bytes=67043328
        ),
    )(queries, keys, values, out_weight)


def solution(mesh):
    C, N = mesh.shape["context"], mesh.shape["tensor"]
    return jax.shard_map(
        functools.partial(body, C, N),
        mesh=mesh,
        in_specs=(
            P(("parts", "context"), "tensor"),
            P(("parts", "context"), "tensor"),
            P(("parts", "context"), "tensor"),
            P("tensor", None),
        ),
        out_specs=P(("parts", "context"), "tensor"),
        check_vma=False,
    )
```
